32 devices in a mesh: grp: 2 (over x), seq: 8 (over z, y), mdl: 2 (over core).
Axes of the slice: x: 2, y: 2, z: 4, core: 2. Of those that a mesh axis runs over, the one named last changes fastest.
Arguments:
- signal: float32 [8, 128, 8192], P('grp', 'mdl', 'seq'), parts along dimension 0, may hold values from -6 to 6
- lengths: int32 [8], P('grp'), parts along dimension 0, may hold values from 1 to 64, 160 in all
- chan_weight: bfloat16 [128, 128, 16], P('mdl'), may hold values from -0.5 to 0.5
- up_weight: bfloat16 [4, 2048, 4096], P(None, 'seq', 'mdl'), may hold values from -0.125 to 0.125
- down_weight: bfloat16 [4, 2048, 4096], P(None, 'seq', 'mdl'), may hold values from -0.09375 to 0.09375
Outputs:
- features: bfloat16 [8, 64, 2048], P(('grp', 'mdl'), 'seq'), parts along dimension 0
The draws below stay inside these ranges and needn't reach their ends.
There are 2 independent parts, one for each index of `grp`. The reference program is written for one: setup_inputs(seed, part) draws one part's arguments, and reference() takes and returns one part's arrays. A program takes and returns all parts, laid end to end along the dimension named above; an argument that names none is the same for every part. Nothing has to cross between parts.
Inputs may be any that keep to these rules, and one draw needn't show every extreme that they name: `lengths`: live windows of each recording; one recording is live for all 64, and all recordings together have (320) // 2.
All inputs are finite; a program needn't handle non-finite values.
Results may differ from the reference program's by a relative error of at most 0.014.
Values may be sent and summed in bfloat16 or wider, within the bound.
A program may use at most 128 MiB of HBM per device.

```python
import math
from functools import partial
import jax
import jax.numpy as jnp
import numpy as np
from jax import lax

D = 2048
FF = 4096
CH = 128
HOP = 128
NLAYER = 4
STREAMS = 4
EMB = 16
FRAMES = 64
SAMPLES = 8192


def block_scale(rng, dims, split, low, largest):
    factor_of, own = 1.0, jax.random.fold_in(rng, 6)
    for position, blocks in split:
        heights = jnp.exp(jax.random.uniform(jax.random.fold_in(own, position), (blocks,), jnp.float32, low / len(split), largest / len(split)))
        factor_of = factor_of * jnp.repeat(heights, dims[position] // blocks).reshape([-1 if axis == position else 1 for axis in range(len(dims))])
    return factor_of


def split_up(count, total, limit, slope):
    loads = [(1 << 20) // math.isqrt(standing ** slope) + 1 for standing in range(2, count + 1)]
    surplus, given = total - limit - (count - 1), [1] * (count - 1)
    while surplus > 0:
        candidates = [i for i in range(count - 1) if given[i] < limit]
        mass, budget = sum([loads[i] for i in candidates]), surplus
        for i in candidates:
            more = min(limit - given[i], max(1, budget * loads[i] // mass), surplus)
            given[i] = given[i] + more
            surplus = surplus - more
    return np.array([limit] + given)


def uneven(key, amount, total, limit, slope):
    if amount == 2:
        one = jax.random.randint(key, (), max(1, total - limit), min(limit, total - 1) + 1)
        return jnp.stack([one, total - one])
    sizes = jnp.asarray(split_up(amount, total, limit, slope), jnp.int32)
    couples = (amount - 1) // 2
    donor, receiver = sizes[1:1 + 2 * couples:2], sizes[2:2 + 2 * couples:2]
    slack = jnp.minimum(donor - 1, limit - receiver)
    passed = jax.random.randint(jax.random.fold_in(key, 1), (couples,), 0, 1 << 20) % (slack + 1)
    sizes = sizes.at[1:1 + 2 * couples:2].set(donor - passed).at[2:2 + 2 * couples:2].set(receiver + passed)
    return sizes[jax.random.permutation(jax.random.fold_in(key, 2), amount)]


def bell_draw(stream_key, shape, spread, reach, split=(), held_as=jnp.bfloat16):
    drawn = jax.random.normal(stream_key, shape, jnp.float32) * spread
    if len(split) > 0:
        drawn = block_scale(stream_key, shape, split, -0.22, 0.18) * drawn
    return jnp.clip(drawn, min=-reach, max=reach).astype(held_as)


def setup_inputs(seed: int = 0, part: int = 0) -> dict:
    arg_keys = jax.random.split(jax.random.key(seed), 6)
    own_keys = jax.random.split(jax.random.fold_in(arg_keys[5], part), 6)
    signal = bell_draw(own_keys[0], (STREAMS, CH, SAMPLES), 1.0, 6.0, ((1, 2), (2, 8)), jnp.float32)
    lengths = uneven(own_keys[1], STREAMS, (STREAMS + 1) * FRAMES // 2, FRAMES, 1).astype(jnp.int32)
    chan_weight = bell_draw(arg_keys[2], (CH, HOP, EMB), HOP ** -0.5, 0.5, ((0, 2),))
    up_weight = bell_draw(arg_keys[3], (NLAYER, D, FF), D ** -0.5, 0.125, ((1, 8), (2, 2)))
    down_weight = bell_draw(arg_keys[4], (NLAYER, D, FF), FF ** -0.5, 0.09375, ((1, 8), (2, 2)))
    return dict(signal=signal, lengths=lengths, chan_weight=chan_weight, up_weight=up_weight, down_weight=down_weight)


EPSILON = 1e-06

def spectral_table(half_span):
    full_span = 2 * half_span
    row_index = jnp.arange(full_span, dtype=jnp.int32)
    col_index = jnp.arange(half_span, dtype=jnp.int32)
    phases = row_index[:, None] * col_index[None, :] % full_span
    angles = phases.astype(jnp.float32) * (2.0 * math.pi / full_span)
    window_taper = 0.5 - 0.5 * jnp.cos(row_index.astype(jnp.float32) * (2.0 * math.pi / full_span))
    weighting = window_taper * (1.0 / math.sqrt(full_span))
    joined = jnp.concatenate([jnp.cos(angles), -jnp.sin(angles)], axis=1) * weighting[:, None]
    return jnp.concatenate([joined[:half_span], joined[half_span:]], axis=1)

def log_power(spectrum):
    half_span = spectrum.shape[-1] // 2
    real_part = spectrum[..., :half_span]
    imag_part = spectrum[..., half_span:]
    return jnp.log1p(real_part * real_part + imag_part * imag_part).astype(jnp.bfloat16)

def stream_spectra(waveform, dft_table):
    padded = jnp.concatenate([waveform, jnp.zeros((waveform.shape[0], HOP), jnp.float32)], axis=1)
    blocks = padded.reshape(waveform.shape[0], FRAMES + 1, HOP)
    products = jnp.dot(blocks, dft_table, precision=lax.Precision.HIGHEST)
    spectrum = products[:, :-1, :2 * HOP] + products[:, 1:, 2 * HOP:]
    return log_power(spectrum)

def normalize(state_rows):
    values = state_rows.astype(jnp.float32)
    scaled = values * lax.rsqrt(lax.optimization_barrier(jnp.mean(values * values, axis=1, keepdims=True)) + EPSILON)
    return (values, scaled.astype(jnp.bfloat16))

def apply_layer(state_rows, up_part, down_part):
    values, normed = normalize(state_rows)
    hidden = jax.nn.gelu(jnp.dot(normed, up_part, preferred_element_type=jnp.float32)).astype(jnp.bfloat16)
    narrowed = lax.dot_general(hidden, down_part, (((1,), (1,)), ((), ())), preferred_element_type=jnp.float32)
    return (values + narrowed).astype(jnp.bfloat16)

def reference(signal, lengths, chan_weight, up_weight, down_weight):
    dft_table = spectral_table(HOP)
    logpower = lax.map(partial(stream_spectra, dft_table=dft_table), signal)
    embedded = jnp.einsum('scfb,cbe->sfce', logpower.astype(jnp.float32), chan_weight.astype(jnp.float32))
    embedded = embedded.reshape(STREAMS, FRAMES, D)
    frame_index = jnp.arange(FRAMES, dtype=jnp.int32)
    live_mask = frame_index[None, :] < lengths[:, None]
    tokens = jnp.where(live_mask[:, :, None], embedded, 0.0).astype(jnp.bfloat16)
    state_rows = tokens.reshape(STREAMS * FRAMES, D)
    for layer_number in range(NLAYER):
        state_rows = apply_layer(state_rows, up_weight[layer_number], down_weight[layer_number])
    return state_rows.reshape(STREAMS, FRAMES, D)
```

```python
import math

import jax
import jax.numpy as jnp
from jax import lax
from jax.sharding import PartitionSpec as P

HOP = 128


EPSILON = 1e-06


def shifted(x, axis, by):
    size = lax.axis_size(axis)
    pairs = [(i, i + by) for i in range(size) if 0 <= i + by < size]
    return lax.ppermute(x, axis, pairs)


def spectral_table(half_span):
    full_span = 2 * half_span
    row_index = jnp.arange(full_span, dtype=jnp.int32)
    col_index = jnp.arange(half_span, dtype=jnp.int32)
    phases = row_index[:, None] * col_index[None, :] % full_span
    angles = phases.astype(jnp.float32) * (2.0 * math.pi / full_span)
    window_taper = 0.5 - 0.5 * jnp.cos(row_index.astype(jnp.float32) * (2.0 * math.pi / full_span))
    weighting = window_taper * (1.0 / math.sqrt(full_span))
    joined = jnp.concatenate([jnp.cos(angles), -jnp.sin(angles)], axis=1) * weighting[:, None]
    return jnp.concatenate([joined[:half_span], joined[half_span:]], axis=1)


def log_power(spectrum):
    half_span = spectrum.shape[-1] // 2
    real_part = spectrum[..., :half_span]
    imag_part = spectrum[..., half_span:]
    return jnp.log1p(real_part * real_part + imag_part * imag_part).astype(jnp.bfloat16)


def project_down(hidden, own_down):
    return lax.dot_general(
        hidden, own_down, (((1,), (1,)), ((), ())), preferred_element_type=jnp.float32
    )


def apply_layer(state, up_rows, down_rows, width):
    values = state.astype(jnp.float32)
    squares = lax.psum(jnp.sum(values * values, axis=1, keepdims=True), "seq")
    partial = jnp.dot(state, up_rows, preferred_element_type=jnp.float32).astype(jnp.bfloat16)
    summed = lax.psum_scatter(partial, "seq", scatter_dimension=1, tiled=True)
    scale = lax.rsqrt(squares * (1.0 / width) + EPSILON)
    hidden = jax.nn.gelu(summed.astype(jnp.float32) * scale).astype(jnp.bfloat16)
    hidden = lax.all_gather(hidden, "seq", axis=1, tiled=True)
    added = lax.psum(project_down(hidden, down_rows), "mdl")
    return (values + added).astype(jnp.bfloat16)


def body(signal, lengths, chan_weight, up_weight, down_weight):
    streams, channels, samples = signal.shape
    frames = samples // HOP
    dft_table = spectral_table(HOP)
    boundary = shifted(signal[:, :, :HOP], "seq", -1)
    local_part = jnp.dot(
        signal.reshape(streams, channels, frames, HOP), dft_table, precision=lax.Precision.HIGHEST
    )
    edge_part = jnp.dot(boundary, dft_table[:, 2 * HOP :], precision=lax.Precision.HIGHEST)
    following = jnp.concatenate([local_part[:, :, 1:, 2 * HOP :], edge_part[:, :, None, :]], axis=2)
    spectrum = local_part[..., : 2 * HOP] + following
    logpower = log_power(spectrum)
    embedded = jnp.einsum(
        "scfb,cbe->sfce", logpower, chan_weight, preferred_element_type=jnp.float32
    )
    embedded = embedded.reshape(streams, frames, channels * chan_weight.shape[2])
    frame_index = lax.axis_index("seq") * frames + jnp.arange(frames, dtype=jnp.int32)
    live_mask = frame_index[None, :] < lengths[:, None]
    tokens = jnp.where(live_mask[:, :, None], embedded, 0.0).astype(jnp.bfloat16)
    rows = lax.all_gather(tokens.reshape(streams * frames, -1), "mdl", axis=1, tiled=True)
    state = lax.all_to_all(rows, "seq", split_axis=1, concat_axis=0, tiled=True)
    width = rows.shape[1]
    for layer in range(up_weight.shape[0]):
        state = apply_layer(state, up_weight[layer], down_weight[layer], width)
    rows = lax.all_to_all(state, "seq", split_axis=0, concat_axis=1, tiled=True)
    full_rows = rows.reshape(streams, frames, width)
    half_streams = streams // lax.axis_size("mdl")
    return lax.dynamic_slice_in_dim(
        full_rows, lax.axis_index("mdl") * half_streams, half_streams, 0
    )


def solution(mesh):
    return jax.shard_map(
        body,
        mesh=mesh,
        in_specs=(
            P("grp", "mdl", "seq"),
            P("grp"),
            P("mdl", None, None),
            P(None, "seq", "mdl"),
            P(None, "seq", "mdl"),
        ),
        out_specs=P(("grp", "mdl"), "seq", None),
        check_vma=False,
    )
```

```python
import math
from functools import partial

import jax
import jax.numpy as jnp
from jax import lax
from jax.experimental import pallas as pl
from jax.experimental.pallas import tpu as pltpu
from jax.sharding import PartitionSpec as P

MESH = pl.DeviceIdType.MESH

HOP = 128


EPSILON = 1e-06


def shifted(x, axis, by):
    size = lax.axis_size(axis)
    pairs = [(i, i + by) for i in range(size) if 0 <= i + by < size]
    return lax.ppermute(x, axis, pairs)


def spectral_table(half_span):
    full_span = 2 * half_span
    row_index = jnp.arange(full_span, dtype=jnp.int32)
    col_index = jnp.arange(half_span, dtype=jnp.int32)
    phases = row_index[:, None] * col_index[None, :] % full_span
    angles = phases.astype(jnp.float32) * (2.0 * math.pi / full_span)
    window_taper = 0.5 - 0.5 * jnp.cos(row_index.astype(jnp.float32) * (2.0 * math.pi / full_span))
    weighting = window_taper * (1.0 / math.sqrt(full_span))
    joined = jnp.concatenate([jnp.cos(angles), -jnp.sin(angles)], axis=1) * weighting[:, None]
    return jnp.concatenate([joined[:half_span], joined[half_span:]], axis=1)


def log_power(spectrum):
    half_span = spectrum.shape[-1] // 2
    real_part = spectrum[..., :half_span]
    imag_part = spectrum[..., half_span:]
    return jnp.log1p(real_part * real_part + imag_part * imag_part).astype(jnp.bfloat16)


def project_down(hidden, own_down):
    return lax.dot_general(
        hidden, own_down, (((1,), (1,)), ((), ())), preferred_element_type=jnp.float32
    )


def apply_layer(state, up_rows, down_rows, width):
    values = state.astype(jnp.float32)
    squares = lax.psum(jnp.sum(values * values, axis=1, keepdims=True), "seq")
    partial = jnp.dot(state, up_rows, preferred_element_type=jnp.float32).astype(jnp.bfloat16)
    summed = lax.psum_scatter(partial, "seq", scatter_dimension=1, tiled=True)
    scale = lax.rsqrt(squares * (1.0 / width) + EPSILON)
    hidden = jax.nn.gelu(summed.astype(jnp.float32) * scale).astype(jnp.bfloat16)
    hidden = lax.all_gather(hidden, "seq", axis=1, tiled=True)
    added = lax.psum(project_down(hidden, down_rows), "mdl")
    return (values + added).astype(jnp.bfloat16)


def exchange_kernel(
    sizes,
    tok_ref, pick_ref, place_ref, up_hbm, down_hbm, out_ref,
    up_v, down_v, arrived, x_v, sq_v, y_out, y_in, z_out, z_in, hid, pair_out, pair_in, fin_out, fin_in,
    up_sem, down_sem, in_send, in_recv, sq_send, sq_recv, ys, yr, zs, zr, hzs, hzr, hys, hyr, ps, pr, fs, fr,
):
    n, layers, live, dq, fq, width = sizes
    nz = n // 2
    s = lax.axis_index("seq")
    m = lax.axis_index("mdl")
    z, y = s // 2, s % 2
    mate = z * 2 + (1 - y)
    me = s * 2 + m

    loads = []
    for k in range(layers):
        loads.append(pltpu.make_async_copy(up_hbm.at[k], up_v.at[k], up_sem.at[k]))
        loads.append(pltpu.make_async_copy(down_hbm.at[k], down_v.at[k], down_sem.at[k]))
    for load in loads:
        load.start()
    sq_v[...] = jnp.zeros_like(sq_v)

    barrier = pltpu.get_barrier_semaphore()
    for d in range(1, 2 * n):
        other = lax.rem(me + d, 2 * n)
        pl.semaphore_signal(
            barrier, inc=1, device_id={"seq": other // 2, "mdl": other % 2}, device_id_type=MESH
        )
    pl.semaphore_wait(barrier, 2 * n - 1)

    def remote(src, dst, send, recv, seq, mdl):
        return pltpu.make_async_remote_copy(
            src_ref=src, dst_ref=dst, send_sem=send, recv_sem=recv,
            device_id={"seq": seq, "mdl": mdl}, device_id_type=MESH,
        )

    def token_copy(j, m2):
        return remote(
            tok_ref.at[:, j * dq : (j + 1) * dq], arrived.at[s],
            in_send.at[2 * j + m2], in_recv.at[s], m * nz + j, m2,
        )

    for j in range(nz):
        for m2 in range(2):
            own = ((m * nz + j) * 2 + m2) == me

            @pl.when(jnp.logical_not(own))
            def _():
                token_copy(j, m2).start()

            @pl.when(own)
            def _():
                pltpu.make_async_copy(
                    tok_ref.at[:, j * dq : (j + 1) * dq], arrived.at[s], in_recv.at[s]
                ).start()

    for src in range(n):
        pltpu.make_async_copy(arrived.at[src], arrived.at[src], in_recv.at[src]).wait()
    for j in range(nz):
        for m2 in range(2):

            @pl.when(((m * nz + j) * 2 + m2) != me)
            def _():
                token_copy(j, m2).wait_send()

    gathered = arrived[...].reshape(pick_ref.shape[1], dq)
    x_v[...] = jnp.dot(pick_ref[...], gathered, preferred_element_type=jnp.float32).astype(jnp.bfloat16)

    order = list(range(1, nz)) + [0]

    def layer(k, carry):
        x = x_v[...]
        xf = x.astype(jnp.float32)
        ones = jnp.ones((8, dq), jnp.float32)
        sq_v[k, 0, :, :live] = lax.dot_general(
            ones, xf * xf, (((1,), (1,)), ((), ())),
            precision=lax.Precision.HIGHEST, preferred_element_type=jnp.float32,
        )
        sq_copies = [
            remote(sq_v.at[k, 0], sq_v.at[k, d], sq_send.at[k, d], sq_recv.at[k, d], lax.rem(s + d, n), m)
            for d in range(1, n)
        ]

        @pl.when(k < 1)
        def _():
            for kk in range(layers):
                pltpu.make_async_copy(up_hbm.at[kk], up_v.at[kk], up_sem.at[kk]).wait()
                pltpu.make_async_copy(down_hbm.at[kk], down_v.at[kk], down_sem.at[kk]).wait()

        def up_part(t, col):
            block = (lax.rem(z + t, nz) * 2 + col) * fq
            return jnp.dot(
                x, up_v[k, :, pl.ds(pl.multiple_of(block, fq), fq)], preferred_element_type=jnp.float32
            )

        y_copies = [
            remote(y_out.at[t], y_in.at[k, t], ys.at[k, t], yr.at[k, t], mate, m) for t in range(nz)
        ]
        for t in order:
            y_out[t] = up_part(t, 1 - y).astype(jnp.bfloat16)
            y_copies[t].start()
            if t == 1:
                for c in sq_copies:
                    c.start()
        z_copies = {
            t: remote(
                z_out.at[t], z_in.at[k, t], zs.at[k, t], zr.at[k, t], lax.rem(z + t, nz) * 2 + y, m
            )
            for t in range(1, nz)
        }
        acc = None
        for t in order:
            mine = up_part(t, y)
            y_copies[t].wait_recv()
            both = mine + y_in[k, t].astype(jnp.float32)
            if t:
                z_out[t] = both.astype(jnp.bfloat16)
                z_copies[t].start()
            else:
                acc = both
        for c in sq_copies:
            c.wait_recv()
        total = sq_v[k, 0]
        for d in range(1, n):
            total = total + sq_v[k, d]
        scale = lax.rsqrt(total * (1.0 / width) + EPSILON)
        scale = scale.T[:live, :1]
        for t in range(1, nz):
            z_copies[t].wait_recv()
            acc = acc + z_in[k, t].astype(jnp.float32)
        v = acc * scale
        hid[k, 0, 0] = (
            0.5 * v * (1.0 + jnp.tanh(0.7978845608 * (v + 0.044715 * (v * v * v))))
        ).astype(jnp.bfloat16)

        hz = {
            t: remote(
                hid.at[k, 0, 0], hid.at[k, 0, t], hzs.at[k, t], hzr.at[k, t],
                lax.rem(z + t, nz) * 2 + y, m,
            )
            for t in range(1, nz)
        }
        hy = [
            remote(hid.at[k, 0, t], hid.at[k, 1, t], hys.at[k, t], hyr.at[k, t], mate, m)
            for t in range(nz)
        ]
        for t in range(1, nz):
            hz[t].start()
        hy[0].start()

        def down_part(t, row, col):
            block = (lax.rem(z - t + nz, nz) * 2 + col) * fq
            return lax.dot_general(
                hid[k, row, t], down_v[k, :, pl.ds(pl.multiple_of(block, fq), fq)],
                (((1,), (1,)), ((), ())), preferred_element_type=jnp.float32,
            )

        summed = down_part(0, 0, y)
        for t in range(1, nz):
            hz[t].wait_recv()
            hy[t].start()
            summed = summed + down_part(t, 0, y)
        for t in range(nz):
            hy[t].wait_recv()
            summed = summed + down_part(t, 1, 1 - y)
        pair_out[...] = summed
        pair = remote(pair_out, pair_in.at[k], ps.at[k], pr.at[k], s, 1 - m)
        pair.start()
        for c in sq_copies + y_copies + hy + list(z_copies.values()) + list(hz.values()):
            c.wait_send()
        pair.wait_recv()
        x_v[...] = (xf + (summed + pair_in[k])).astype(jnp.bfloat16)
        pair.wait_send()
        return carry

    lax.fori_loop(0, layers, layer, 0)

    spread = jnp.dot(place_ref[...], x_v[...], preferred_element_type=jnp.float32).astype(jnp.bfloat16)
    fin_out[...] = spread.reshape(fin_out.shape)
    fin_in[0] = fin_out[s]
    copies = []
    for d in range(1, n):
        dest = lax.rem(s + d, n)
        copies.append(remote(fin_out.at[dest], fin_in.at[d], fs.at[d], fr.at[d], dest, m))
        copies[-1].start()
    out_ref[:, pl.ds(pl.multiple_of(s * dq, dq), dq)] = fin_in[0]
    for d in range(1, n):
        copies[d - 1].wait_recv()
        src = lax.rem(s - d + n, n)
        out_ref[:, pl.ds(pl.multiple_of(src * dq, dq), dq)] = fin_in[d]
    for c in copies:
        c.wait_send()


def selection(lengths, streams, frames, n, live):
    total = streams * frames * n
    spot = jnp.arange(total, dtype=jnp.int32)
    frame = (spot // (streams * frames)) * frames + spot % frames
    stream = spot // frames % streams
    rank = frame
    limit = jnp.zeros_like(spot)
    for i in range(streams):
        rank = rank + jnp.where(stream > i, lengths[i], 0)
        limit = limit + jnp.where(stream == i, lengths[i], 0)
    rank = jnp.where(frame < limit, rank, -1)
    return rank


def run_layers(tokens, lengths, up_weight, down_weight, live):
    streams, frames, half = tokens.shape
    n = lax.axis_size("seq")
    layers, dq, ff = up_weight.shape
    fq = ff // n
    nz = n // 2
    width = dq * n
    rows = streams * frames
    rank = selection(lengths, streams, frames, n, live)
    slot = jnp.arange(live, dtype=jnp.int32)
    pick = (slot[:, None] == rank[None, :]).astype(jnp.bfloat16)
    kept = lax.dynamic_slice_in_dim(
        rank.reshape(n, 2, rows // 2), lax.axis_index("mdl"), 1, 1
    ).reshape(n * rows // 2)
    place = (kept[:, None] == slot[None, :]).astype(jnp.bfloat16)
    sizes = (n, layers, live, dq, fq, width)
    bf, f32, dma = jnp.bfloat16, jnp.float32, pltpu.SemaphoreType.DMA
    vmem = pl.BlockSpec(memory_space=pltpu.VMEM)
    lanes = -(-live // 128) * 128
    out = pl.pallas_call(
        partial(exchange_kernel, sizes),
        out_shape=jax.ShapeDtypeStruct((rows // 2, width), bf),
        in_specs=[vmem, vmem, vmem, pl.BlockSpec(memory_space=pl.ANY), pl.BlockSpec(memory_space=pl.ANY)],
        out_specs=vmem,
        scratch_shapes=[
            pltpu.VMEM((layers, dq, ff), bf),
            pltpu.VMEM((layers, dq, ff), bf),
            pltpu.VMEM((n, rows, dq), bf),
            pltpu.VMEM((live, dq), bf),
            pltpu.VMEM((layers, n, 8, lanes), f32),
            pltpu.VMEM((nz, live, fq), bf),
            pltpu.VMEM((layers, nz, live, fq), bf),
            pltpu.VMEM((nz, live, fq), bf),
            pltpu.VMEM((layers, nz, live, fq), bf),
            pltpu.VMEM((layers, 2, nz, live, fq), bf),
            pltpu.VMEM((live, dq), f32),
            pltpu.VMEM((layers, live, dq), f32),
            pltpu.VMEM((n, rows // 2, dq), bf),
            pltpu.VMEM((n, rows // 2, dq), bf),
            dma((layers,)), dma((layers,)),
            dma((n,)), dma((n,)),
            dma((layers, n)), dma((layers, n)),
            dma((layers, nz)), dma((layers, nz)),
            dma((layers, nz)), dma((layers, nz)),
            dma((layers, nz)), dma((layers, nz)),
            dma((layers, nz)), dma((layers, nz)),
            dma((layers,)), dma((layers,)),
            dma((n,)), dma((n,)),
        ],
        compiler_params=pltpu.CompilerParams(
            collective_id=0, has_side_effects=True, vmem_limit_bytes=48 * 1024 * 1024
        ),
        name="exchange",
    )(tokens.reshape(rows, half), pick, place, up_weight, down_weight)
    return out.reshape(streams // 2, frames, width)


def body(signal, lengths, chan_weight, up_weight, down_weight):
    streams, channels, samples = signal.shape
    frames = samples // HOP
    dft_table = spectral_table(HOP)
    boundary = shifted(signal[:, :, :HOP], "seq", -1)
    local_part = jnp.dot(
        signal.reshape(streams, channels, frames, HOP), dft_table, precision=lax.Precision.HIGHEST
    )
    edge_part = jnp.dot(boundary, dft_table[:, 2 * HOP :], precision=lax.Precision.HIGHEST)
    following = jnp.concatenate([local_part[:, :, 1:, 2 * HOP :], edge_part[:, :, None, :]], axis=2)
    spectrum = local_part[..., : 2 * HOP] + following
    logpower = log_power(spectrum)
    embedded = jnp.einsum(
        "scfb,cbe->sfce", logpower, chan_weight, preferred_element_type=jnp.float32
    )
    embedded = embedded.reshape(streams, frames, channels * chan_weight.shape[2])
    shards = lax.axis_size("seq")
    live = (streams + 1) * frames * shards // 2
    blocks = (up_weight.shape[1], up_weight.shape[2] // shards)
    if lax.axis_size("mdl") == 2 and shards % 2 == 0 and all(b % 128 == 0 for b in blocks) and live % 16 == 0:
        return run_layers(embedded.astype(jnp.bfloat16), lengths, up_weight, down_weight, live)
    frame_index = lax.axis_index("seq") * frames + jnp.arange(frames, dtype=jnp.int32)
    live_mask = frame_index[None, :] < lengths[:, None]
    tokens = jnp.where(live_mask[:, :, None], embedded, 0.0).astype(jnp.bfloat16)
    rows = lax.all_gather(tokens.reshape(streams * frames, -1), "mdl", axis=1, tiled=True)
    state = lax.all_to_all(rows, "seq", split_axis=1, concat_axis=0, tiled=True)
    width = rows.shape[1]
    for layer in range(up_weight.shape[0]):
        state = apply_layer(state, up_weight[layer], down_weight[layer], width)
    rows = lax.all_to_all(state, "seq", split_axis=0, concat_axis=1, tiled=True)
    full_rows = rows.reshape(streams, frames, width)
    half_streams = streams // lax.axis_size("mdl")
    return lax.dynamic_slice_in_dim(
        full_rows, lax.axis_index("mdl") * half_streams, half_streams, 0
    )


def solution(mesh):
    return jax.shard_map(
        body,
        mesh=mesh,
        in_specs=(
            P("grp", "mdl", "seq"),
            P("grp"),
            P("mdl", None, None),
            P(None, "seq", "mdl"),
            P(None, "seq", "mdl"),
        ),
        out_specs=P(("grp", "mdl"), "seq", None),
        check_vma=False,
    )
```

```python
import math
from functools import partial

import jax
import jax.numpy as jnp
from jax import lax
from jax.experimental import pallas as pl
from jax.experimental.pallas import tpu as pltpu
from jax.sharding import PartitionSpec as P

MESH = pl.DeviceIdType.MESH
CHUNKS = 2

HOP = 128


EPSILON = 1e-06


def shifted(x, axis, by):
    size = lax.axis_size(axis)
    pairs = [(i, i + by) for i in range(size) if 0 <= i + by < size]
    return lax.ppermute(x, axis, pairs)


def spectral_table(half_span):
    full_span = 2 * half_span
    row_index = jnp.arange(full_span, dtype=jnp.int32)
    col_index = jnp.arange(half_span, dtype=jnp.int32)
    phases = row_index[:, None] * col_index[None, :] % full_span
    angles = phases.astype(jnp.float32) * (2.0 * math.pi / full_span)
    window_taper = 0.5 - 0.5 * jnp.cos(row_index.astype(jnp.float32) * (2.0 * math.pi / full_span))
    weighting = window_taper * (1.0 / math.sqrt(full_span))
    joined = jnp.concatenate([jnp.cos(angles), -jnp.sin(angles)], axis=1) * weighting[:, None]
    return jnp.concatenate([joined[:half_span], joined[half_span:]], axis=1)


def log_power(spectrum):
    half_span = spectrum.shape[-1] // 2
    real_part = spectrum[..., :half_span]
    imag_part = spectrum[..., half_span:]
    return jnp.log1p(real_part * real_part + imag_part * imag_part).astype(jnp.bfloat16)


def project_down(hidden, own_down):
    return lax.dot_general(
        hidden, own_down, (((1,), (1,)), ((), ())), preferred_element_type=jnp.float32
    )


def apply_layer(state, up_rows, down_rows, width):
    values = state.astype(jnp.float32)
    squares = lax.psum(jnp.sum(values * values, axis=1, keepdims=True), "seq")
    partial = jnp.dot(state, up_rows, preferred_element_type=jnp.float32).astype(jnp.bfloat16)
    summed = lax.psum_scatter(partial, "seq", scatter_dimension=1, tiled=True)
    scale = lax.rsqrt(squares * (1.0 / width) + EPSILON)
    hidden = jax.nn.gelu(summed.astype(jnp.float32) * scale).astype(jnp.bfloat16)
    hidden = lax.all_gather(hidden, "seq", axis=1, tiled=True)
    added = lax.psum(project_down(hidden, down_rows), "mdl")
    return (values + added).astype(jnp.bfloat16)


def exchange_kernel(
    sizes,
    len_ref, tok_ref, up_hbm, down_hbm, out_ref,
    up_v, down_v, arrived, x_v, sq_v, y_out, y_in, z_out, z_in, hid, pair_out, pair_in, fin_out, fin_in,
    up_sem, down_sem, in_send, in_recv, ys, yr, zs, zr, hzs, hzr, hys, hyr, ps, pr, fs, fr,
):
    n, layers, streams, frames, live, dq, fq, width = sizes
    nz = n // 2
    rows = streams * frames
    ch = live // CHUNKS
    s = lax.axis_index("seq")
    m = lax.axis_index("mdl")
    z, y = s // 2, s % 2
    mate = z * 2 + (1 - y)
    me = s * 2 + m

    def rank_of(stream, frame):
        rank, limit = frame, jnp.zeros_like(frame)
        for i in range(streams):
            rank = rank + jnp.where(stream > i, len_ref[i], 0)
            limit = limit + jnp.where(stream == i, len_ref[i], 0)
        return jnp.where(frame < limit, rank, -1)

    loads = []
    for k in range(layers):
        loads.append(pltpu.make_async_copy(up_hbm.at[k], up_v.at[k], up_sem.at[k]))
        loads.append(pltpu.make_async_copy(down_hbm.at[k], down_v.at[k], down_sem.at[k]))
    for load in loads:
        load.start()
    y_out[...] = jnp.zeros_like(y_out)
    z_out[...] = jnp.zeros_like(z_out)
    sq_v[...] = jnp.zeros_like(sq_v)

    barrier = pltpu.get_barrier_semaphore()
    for d in range(1, 2 * n):
        other = lax.rem(me + d, 2 * n)
        pl.semaphore_signal(
            barrier, inc=1, device_id={"seq": other // 2, "mdl": other % 2}, device_id_type=MESH
        )
    pl.semaphore_wait(barrier, 2 * n - 1)

    def remote(src, dst, send, recv, seq, mdl):
        return pltpu.make_async_remote_copy(
            src_ref=src, dst_ref=dst, send_sem=send, recv_sem=recv,
            device_id={"seq": seq, "mdl": mdl}, device_id_type=MESH,
        )

    def token_copy(j, m2):
        return remote(
            tok_ref.at[:, j * dq : (j + 1) * dq], arrived.at[s],
            in_send.at[2 * j + m2], in_recv.at[s], m * nz + j, m2,
        )

    for j in range(nz):
        for m2 in range(2):
            own = ((m * nz + j) * 2 + m2) == me

            @pl.when(jnp.logical_not(own))
            def _():
                token_copy(j, m2).start()

            @pl.when(own)
            def _():
                pltpu.make_async_copy(
                    tok_ref.at[:, j * dq : (j + 1) * dq], arrived.at[s], in_recv.at[s]
                ).start()

    for src in range(n):
        pltpu.make_async_copy(arrived.at[src], arrived.at[src], in_recv.at[src]).wait()
    for j in range(nz):
        for m2 in range(2):

            @pl.when(((m * nz + j) * 2 + m2) != me)
            def _():
                token_copy(j, m2).wait_send()

    spot = lax.broadcasted_iota(jnp.int32, (1, n * rows), 1)
    rank = rank_of(spot // frames % streams, spot // rows * frames + spot % frames)
    slot = lax.broadcasted_iota(jnp.int32, (live, n * rows), 0)
    pick = jnp.where(slot == rank, 1.0, 0.0).astype(jnp.bfloat16)
    gathered = arrived[...].reshape(n * rows, dq)
    x_v[...] = (
        jnp.dot(pick, gathered, preferred_element_type=jnp.float32)
        .astype(jnp.bfloat16)
        .reshape(CHUNKS, ch, dq)
    )
    for load in loads:
        load.wait()

    order = list(range(1, nz)) + [0]
    tail = sq_v.shape[-1]

    def up_part(k, x, t, col):
        block = (lax.rem(z + t, nz) * 2 + col) * fq
        return jnp.dot(
            x, up_v[k, :, pl.ds(pl.multiple_of(block, fq), fq)], preferred_element_type=jnp.float32
        )

    def y_copy(k, c, t):
        i = k * CHUNKS + c
        return remote(y_out.at[c, t], y_in.at[i, t], ys.at[i, t], yr.at[i, t], mate, m)

    def z_copy(k, c, t):
        i = k * CHUNKS + c
        return remote(
            z_out.at[c, t], z_in.at[i, t], zs.at[i, t], zr.at[i, t], lax.rem(z + t, nz) * 2 + y, m
        )

    def hz_copy(k, c, t):
        i = k * CHUNKS + c
        return remote(
            hid.at[i, 0, 0], hid.at[i, 0, t], hzs.at[i, t], hzr.at[i, t], lax.rem(z + t, nz) * 2 + y, m
        )

    def hy_copy(k, c, t):
        i = k * CHUNKS + c
        return remote(hid.at[i, 0, t], hid.at[i, 1, t], hys.at[i, t], hyr.at[i, t], mate, m)

    def pair_copy(k, c):
        i = k * CHUNKS + c
        return remote(pair_out.at[c], pair_in.at[i], ps.at[i], pr.at[i], s, 1 - m)

    def send_up(k, c):
        x = x_v[c]
        xf = x.astype(jnp.float32)
        squares = lax.dot_general(
            jnp.ones((16, dq), jnp.float32), xf * xf, (((1,), (1,)), ((), ())),
            precision=lax.Precision.HIGHEST, preferred_element_type=jnp.float32,
        )
        sq_v[c, :, :ch] = squares
        for t in order:
            y_out[c, t, :ch] = up_part(k, x, t, 1 - y).astype(jnp.bfloat16)
            y_out[c, t, ch:, :ch] = squares.astype(jnp.bfloat16)
            y_copy(k, c, t).start()

    def combine(k, c):
        i = k * CHUNKS + c
        x = x_v[c]
        for t in order:
            mine = up_part(k, x, t, y)
            y_copy(k, c, t).wait_recv()
            both = mine + y_in[i, t, :ch].astype(jnp.float32)
            squares = sq_v[c] + y_in[i, t, ch:, :tail].astype(jnp.float32)
            if t:
                z_out[c, t, :ch] = both.astype(jnp.bfloat16)
                z_out[c, t, ch:, :tail] = squares.astype(jnp.bfloat16)
                z_copy(k, c, t).start()
        return both, squares

    def activate(k, c, both, squares):
        i = k * CHUNKS + c
        for t in range(1, nz):
            z_copy(k, c, t).wait_recv()
            both = both + z_in[i, t, :ch].astype(jnp.float32)
            squares = squares + z_in[i, t, ch:, :tail].astype(jnp.float32)
        scale = lax.rsqrt(squares * (1.0 / width) + EPSILON).T[:ch, :1]
        v = both * scale
        hid[i, 0, 0] = (
            0.5 * v * (1.0 + jnp.tanh(0.7978845608 * (v + 0.044715 * (v * v * v))))
        ).astype(jnp.bfloat16)
        for t in range(1, nz):
            hz_copy(k, c, t).start()
        hy_copy(k, c, 0).start()

    def down_part(k, c, t, row, col):
        block = (lax.rem(z - t + nz, nz) * 2 + col) * fq
        return lax.dot_general(
            hid[k * CHUNKS + c, row, t], down_v[k, :, pl.ds(pl.multiple_of(block, fq), fq)],
            (((1,), (1,)), ((), ())), preferred_element_type=jnp.float32,
        )

    def forward(k, c):
        summed = down_part(k, c, 0, 0, y)
        for t in range(1, nz):
            hz_copy(k, c, t).wait_recv()
            hy_copy(k, c, t).start()
            summed = summed + down_part(k, c, t, 0, y)
        return summed

    def finish(k, c, summed):
        for t in range(nz):
            hy_copy(k, c, t).wait_recv()
            summed = summed + down_part(k, c, t, 1, 1 - y)
        pair_out[c] = summed
        pair_copy(k, c).start()
        for t in range(nz):
            y_copy(k, c, t).wait_send()
            hy_copy(k, c, t).wait_send()
        for t in range(1, nz):
            z_copy(k, c, t).wait_send()
            hz_copy(k, c, t).wait_send()
        pair_copy(k, c).wait_recv()
        x_v[c] = (x_v[c].astype(jnp.float32) + (summed + pair_in[k * CHUNKS + c])).astype(jnp.bfloat16)
        pair_copy(k, c).wait_send()

        @pl.when(k + 1 < layers)
        def _():
            send_up(k + 1, c)

    for c in range(CHUNKS):
        send_up(0, c)

    def layer(k, carry):
        parts = [combine(k, c) for c in range(CHUNKS)]
        for c in range(CHUNKS):
            activate(k, c, *parts[c])
        sums = [forward(k, c) for c in range(CHUNKS)]
        for c in range(CHUNKS):
            finish(k, c, sums[c])
        return carry

    lax.fori_loop(0, layers, layer, 0)

    half = rows // 2
    spot = lax.broadcasted_iota(jnp.int32, (n * half, 1), 0)
    rank = rank_of(m * (streams // 2) + spot // frames % (streams // 2), spot // half * frames + spot % frames)
    slot = lax.broadcasted_iota(jnp.int32, (n * half, live), 1)
    place = jnp.where(slot == rank, 1.0, 0.0).astype(jnp.bfloat16)
    spread = jnp.dot(place, x_v[...].reshape(live, dq), preferred_element_type=jnp.float32).astype(jnp.bfloat16)
    fin_out[...] = spread.reshape(fin_out.shape)
    fin_in[0] = fin_out[s]
    copies = []
    for d in range(1, n):
        dest = lax.rem(s + d, n)
        copies.append(remote(fin_out.at[dest], fin_in.at[d], fs.at[d], fr.at[d], dest, m))
        copies[-1].start()
    out_ref[:, pl.ds(pl.multiple_of(s * dq, dq), dq)] = fin_in[0]
    for d in range(1, n):
        copies[d - 1].wait_recv()
        src = lax.rem(s - d + n, n)
        out_ref[:, pl.ds(pl.multiple_of(src * dq, dq), dq)] = fin_in[d]
    for c in copies:
        c.wait_send()


def run_layers(tokens, lengths, up_weight, down_weight, live):
    streams, frames, half = tokens.shape
    n = lax.axis_size("seq")
    layers, dq, ff = up_weight.shape
    fq = ff // n
    nz = n // 2
    width = dq * n
    rows = streams * frames
    sizes = (n, layers, streams, frames, live, dq, fq, width)
    ch = live // CHUNKS
    slots = layers * CHUNKS
    bf, f32, dma = jnp.bfloat16, jnp.float32, pltpu.SemaphoreType.DMA
    vmem = pl.BlockSpec(memory_space=pltpu.VMEM)
    hbm = pl.BlockSpec(memory_space=pltpu.HBM)
    lanes = -(-ch // 128) * 128
    out = pl.pallas_call(
        partial(exchange_kernel, sizes),
        out_shape=jax.ShapeDtypeStruct((rows // 2, width), bf),
        in_specs=[pl.BlockSpec(memory_space=pltpu.SMEM), vmem, hbm, hbm],
        out_specs=vmem,
        scratch_shapes=[
            pltpu.VMEM((layers, dq, ff), bf),
            pltpu.VMEM((layers, dq, ff), bf),
            pltpu.VMEM((n, rows, dq), bf),
            pltpu.VMEM((CHUNKS, ch, dq), bf),
            pltpu.VMEM((CHUNKS, 16, lanes), f32),
            pltpu.VMEM((CHUNKS, nz, ch + 16, fq), bf),
            pltpu.VMEM((slots, nz, ch + 16, fq), bf),
            pltpu.VMEM((CHUNKS, nz, ch + 16, fq), bf),
            pltpu.VMEM((slots, nz, ch + 16, fq), bf),
            pltpu.VMEM((slots, 2, nz, ch, fq), bf),
            pltpu.VMEM((CHUNKS, ch, dq), f32),
            pltpu.VMEM((slots, ch, dq), f32),
            pltpu.VMEM((n, rows // 2, dq), bf),
            pltpu.VMEM((n, rows // 2, dq), bf),
            dma((layers,)), dma((layers,)),
            dma((n,)), dma((n,)),
            dma((slots, nz)), dma((slots, nz)),
            dma((slots, nz)), dma((slots, nz)),
            dma((slots, nz)), dma((slots, nz)),
            dma((slots, nz)), dma((slots, nz)),
            dma((slots,)), dma((slots,)),
            dma((n,)), dma((n,)),
        ],
        compiler_params=pltpu.CompilerParams(
            collective_id=0, has_side_effects=True, vmem_limit_bytes=48 * 1024 * 1024
        ),
        name="exchange",
    )(lengths, tokens.reshape(rows, half), up_weight, down_weight)
    return out.reshape(streams // 2, frames, width)


def body(signal, lengths, chan_weight, up_weight, down_weight):
    streams, channels, samples = signal.shape
    frames = samples // HOP
    dft_table = spectral_table(HOP)
    boundary = shifted(signal[:, :, :HOP], "seq", -1)
    local_part = jnp.dot(
        signal.reshape(streams, channels, frames, HOP), dft_table, precision=lax.Precision.HIGHEST
    )
    edge_part = jnp.dot(boundary, dft_table[:, 2 * HOP :], precision=lax.Precision.HIGHEST)
    following = jnp.concatenate([local_part[:, :, 1:, 2 * HOP :], edge_part[:, :, None, :]], axis=2)
    spectrum = local_part[..., : 2 * HOP] + following
    logpower = log_power(spectrum)
    embedded = jnp.einsum(
        "scfb,cbe->sfce", logpower, chan_weight, preferred_element_type=jnp.float32
    )
    embedded = embedded.reshape(streams, frames, channels * chan_weight.shape[2])
    shards = lax.axis_size("seq")
    live = (streams + 1) * frames * shards // 2
    blocks = (up_weight.shape[1], up_weight.shape[2] // shards)
    if lax.axis_size("mdl") == 2 and shards % 2 == 0 and all(b % 128 == 0 for b in blocks) and live % (16 * CHUNKS) == 0 and live // CHUNKS <= blocks[1]:
        return run_layers(embedded.astype(jnp.bfloat16), lengths, up_weight, down_weight, live)
    frame_index = lax.axis_index("seq") * frames + jnp.arange(frames, dtype=jnp.int32)
    live_mask = frame_index[None, :] < lengths[:, None]
    tokens = jnp.where(live_mask[:, :, None], embedded, 0.0).astype(jnp.bfloat16)
    rows = lax.all_gather(tokens.reshape(streams * frames, -1), "mdl", axis=1, tiled=True)
    state = lax.all_to_all(rows, "seq", split_axis=1, concat_axis=0, tiled=True)
    width = rows.shape[1]
    for layer in range(up_weight.shape[0]):
        state = apply_layer(state, up_weight[layer], down_weight[layer], width)
    rows = lax.all_to_all(state, "seq", split_axis=0, concat_axis=1, tiled=True)
    full_rows = rows.reshape(streams, frames, width)
    half_streams = streams // lax.axis_size("mdl")
    return lax.dynamic_slice_in_dim(
        full_rows, lax.axis_index("mdl") * half_streams, half_streams, 0
    )


def solution(mesh):
    return jax.shard_map(
        body,
        mesh=mesh,
        in_specs=(
            P("grp", "mdl", "seq"),
            P("grp"),
            P("mdl", None, None),
            P(None, "seq", "mdl"),
            P(None, "seq", "mdl"),
        ),
        out_specs=P(("grp", "mdl"), "seq", None),
        check_vma=False,
    )
```

```python
import math
from functools import partial

import jax
import jax.numpy as jnp
import numpy as np
from jax import lax
from jax.experimental import pallas as pl
from jax.experimental.pallas import tpu as pltpu
from jax.sharding import PartitionSpec as P

MESH = pl.DeviceIdType.MESH
CHUNKS = 2

HOP = 128


EPSILON = 1e-06


def shifted(x, axis, by):
    size = lax.axis_size(axis)
    pairs = [(i, i + by) for i in range(size) if 0 <= i + by < size]
    return lax.ppermute(x, axis, pairs)


def spectral_table(half_span):
    full_span = 2 * half_span
    row_index = np.arange(full_span)
    phases = row_index[:, None] * np.arange(half_span)[None, :] % full_span
    angles = phases * (2.0 * math.pi / full_span)
    window_taper = 0.5 - 0.5 * np.cos(row_index * (2.0 * math.pi / full_span))
    weighting = window_taper * (1.0 / math.sqrt(full_span))
    joined = np.concatenate([np.cos(angles), -np.sin(angles)], axis=1) * weighting[:, None]
    return jnp.asarray(
        np.concatenate([joined[:half_span], joined[half_span:]], axis=1).astype(np.float32)
    )


def log_power(spectrum):
    half_span = spectrum.shape[-1] // 2
    real_part = spectrum[..., :half_span]
    imag_part = spectrum[..., half_span:]
    return jnp.log1p(real_part * real_part + imag_part * imag_part).astype(jnp.bfloat16)


def project_down(hidden, own_down):
    return lax.dot_general(
        hidden, own_down, (((1,), (1,)), ((), ())), preferred_element_type=jnp.float32
    )


def apply_layer(state, up_rows, down_rows, width):
    values = state.astype(jnp.float32)
    squares = lax.psum(jnp.sum(values * values, axis=1, keepdims=True), "seq")
    partial = jnp.dot(state, up_rows, preferred_element_type=jnp.float32).astype(jnp.bfloat16)
    summed = lax.psum_scatter(partial, "seq", scatter_dimension=1, tiled=True)
    scale = lax.rsqrt(squares * (1.0 / width) + EPSILON)
    hidden = jax.nn.gelu(summed.astype(jnp.float32) * scale).astype(jnp.bfloat16)
    hidden = lax.all_gather(hidden, "seq", axis=1, tiled=True)
    added = lax.psum(project_down(hidden, down_rows), "mdl")
    return (values + added).astype(jnp.bfloat16)


def exchange_kernel(
    sizes,
    len_ref, tok_ref, up_hbm, down_hbm, out_ref,
    up_v, down_v, arrived, x_v, sq_v, y_out, y_in, z_out, z_in, hid, pair_out, pair_in, fin_out, fin_in,
    up_sem, down_sem, in_send, in_recv, ys, yr, zs, zr, hzs, hzr, hys, hyr, ps, pr, fs, fr,
):
    n, layers, streams, frames, live, dq, fq, width = sizes
    nz = n // 2
    rows = streams * frames
    ch = live // CHUNKS
    s = lax.axis_index("seq")
    m = lax.axis_index("mdl")
    z, y = s // 2, s % 2
    mate = z * 2 + (1 - y)
    inner = (z == 1) | (z == 2)
    me = s * 2 + m

    def rank_of(stream, frame):
        rank, limit = frame, jnp.zeros_like(frame)
        for i in range(streams):
            rank = rank + jnp.where(stream > i, len_ref[i], 0)
            limit = limit + jnp.where(stream == i, len_ref[i], 0)
        return jnp.where(frame < limit, rank, -1)

    loads = []
    for k in range(layers):
        loads.append(pltpu.make_async_copy(up_hbm.at[k], up_v.at[k], up_sem.at[k]))
        loads.append(pltpu.make_async_copy(down_hbm.at[k], down_v.at[k], down_sem.at[k]))
    for load in loads:
        load.start()
    y_out[...] = jnp.zeros_like(y_out)
    z_out[...] = jnp.zeros_like(z_out)
    sq_v[...] = jnp.zeros_like(sq_v)

    barrier = pltpu.get_barrier_semaphore()
    for d in range(1, 2 * n):
        other = lax.rem(me + d, 2 * n)
        pl.semaphore_signal(
            barrier, inc=1, device_id={"seq": other // 2, "mdl": other % 2}, device_id_type=MESH
        )
    pl.semaphore_wait(barrier, 2 * n - 1)

    def remote(src, dst, send, recv, seq, mdl):
        return pltpu.make_async_remote_copy(
            src_ref=src, dst_ref=dst, send_sem=send, recv_sem=recv,
            device_id={"seq": seq, "mdl": mdl}, device_id_type=MESH,
        )

    def token_copy(j, m2):
        return remote(
            tok_ref.at[:, j * dq : (j + 1) * dq], arrived.at[s],
            in_send.at[2 * j + m2], in_recv.at[s], m * nz + j, m2,
        )

    for j in range(nz):
        for m2 in range(2):
            own = ((m * nz + j) * 2 + m2) == me

            @pl.when(jnp.logical_not(own))
            def _():
                token_copy(j, m2).start()

            @pl.when(own)
            def _():
                pltpu.make_async_copy(
                    tok_ref.at[:, j * dq : (j + 1) * dq], arrived.at[s], in_recv.at[s]
                ).start()

    for src in range(n):
        pltpu.make_async_copy(arrived.at[src], arrived.at[src], in_recv.at[src]).wait()
    for j in range(nz):
        for m2 in range(2):

            @pl.when(((m * nz + j) * 2 + m2) != me)
            def _():
                token_copy(j, m2).wait_send()

    spot = lax.broadcasted_iota(jnp.int32, (1, n * rows), 1)
    rank = rank_of(spot // frames % streams, spot // rows * frames + spot % frames)
    slot = lax.broadcasted_iota(jnp.int32, (live, n * rows), 0)
    pick = jnp.where(slot == rank, 1.0, 0.0).astype(jnp.bfloat16)
    gathered = arrived[...].reshape(n * rows, dq)
    x_v[...] = (
        jnp.dot(pick, gathered, preferred_element_type=jnp.float32)
        .astype(jnp.bfloat16)
        .reshape(CHUNKS, ch, dq)
    )
    for load in loads:
        load.wait()

    order = list(range(1, nz)) + [0]
    tail = sq_v.shape[-1]

    def up_part(k, x, t, col):
        block = (lax.rem(z + t, nz) * 2 + col) * fq
        return jnp.dot(
            x, up_v[k, :, pl.ds(pl.multiple_of(block, fq), fq)], preferred_element_type=jnp.float32
        )

    def y_copy(k, c, t):
        i = k * CHUNKS + c
        return remote(y_out.at[c, t], y_in.at[i, t], ys.at[i, t], yr.at[i, t], mate, m)

    def z_copy(k, c, t):
        i = k * CHUNKS + c
        return remote(
            z_out.at[c, t], z_in.at[i, t], zs.at[i, t], zr.at[i, t], lax.rem(z + t, nz) * 2 + y, m
        )

    def hz_copy(k, c, t):
        i = k * CHUNKS + c
        if nz == 4 and t == 2:
            source = jnp.where(inner, jnp.where(z == 1, 3, 1), 0)
            target = jnp.where(inner, jnp.where(z == 1, 0, 3), lax.rem(z + t, nz))
        else:
            source, target = 0, lax.rem(z + t, nz)
        return remote(
            hid.at[i, 0, source], hid.at[i, 0, t], hzs.at[i, t], hzr.at[i, t], target * 2 + y, m
        )

    def hy_copy(k, c, t):
        i = k * CHUNKS + c
        return remote(hid.at[i, 0, t], hid.at[i, 1, t], hys.at[i, t], hyr.at[i, t], mate, m)

    def pair_copy(k, c):
        i = k * CHUNKS + c
        return remote(pair_out.at[c], pair_in.at[i], ps.at[i], pr.at[i], s, 1 - m)

    def send_up(k, c):
        x = x_v[c]
        xf = x.astype(jnp.float32)
        squares = lax.dot_general(
            jnp.ones((16, dq), jnp.float32), xf * xf, (((1,), (1,)), ((), ())),
            precision=lax.Precision.HIGHEST, preferred_element_type=jnp.float32,
        )
        sq_v[c, :, :ch] = squares
        for t in order:
            y_out[c, t, :ch] = up_part(k, x, t, 1 - y).astype(jnp.bfloat16)
            y_out[c, t, ch:, :ch] = squares.astype(jnp.bfloat16)
            y_copy(k, c, t).start()

    def combine(k, c):
        i = k * CHUNKS + c
        x = x_v[c]
        for t in order:
            mine = up_part(k, x, t, y)
            y_copy(k, c, t).wait_recv()
            both = mine + y_in[i, t, :ch].astype(jnp.float32)
            squares = sq_v[c] + y_in[i, t, ch:, :tail].astype(jnp.float32)
            if t:
                z_out[c, t, :ch] = both.astype(jnp.bfloat16)
                z_out[c, t, ch:, :tail] = squares.astype(jnp.bfloat16)
                z_copy(k, c, t).start()
        return both, squares

    def activate(k, c, both, squares):
        i = k * CHUNKS + c
        for t in range(1, nz):
            z_copy(k, c, t).wait_recv()
            both = both + z_in[i, t, :ch].astype(jnp.float32)
            squares = squares + z_in[i, t, ch:, :tail].astype(jnp.float32)
        scale = lax.rsqrt(squares * (1.0 / width) + EPSILON).T[:ch, :1]
        v = both * scale
        hid[i, 0, 0] = (
            0.5 * v * (1.0 + jnp.tanh(0.7978845608 * (v + 0.044715 * (v * v * v))))
        ).astype(jnp.bfloat16)
        for t in range(1, nz):
            if nz == 4 and t == 2:

                @pl.when(jnp.logical_not(inner))
                def _():
                    hz_copy(k, c, t).start()

            else:
                hz_copy(k, c, t).start()
        hy_copy(k, c, 0).start()

    def down_part(k, c, t, row, col):
        block = (lax.rem(z - t + nz, nz) * 2 + col) * fq
        return lax.dot_general(
            hid[k * CHUNKS + c, row, t], down_v[k, :, pl.ds(pl.multiple_of(block, fq), fq)],
            (((1,), (1,)), ((), ())), preferred_element_type=jnp.float32,
        )

    def forward(k, c):
        summed = down_part(k, c, 0, 0, y)
        for t in (1, 3, 2) if nz == 4 else range(1, nz):
            hz_copy(k, c, t).wait_recv()
            if nz == 4 and t != 2:

                @pl.when(z == (2 if t == 1 else 1))
                def _():
                    hz_copy(k, c, 2).start()

            hy_copy(k, c, t).start()
            summed = summed + down_part(k, c, t, 0, y)
        return summed

    def finish(k, c, summed):
        for t in range(nz):
            hy_copy(k, c, t).wait_recv()
            summed = summed + down_part(k, c, t, 1, 1 - y)
        pair_out[c] = summed
        pair_copy(k, c).start()
        for t in range(nz):
            y_copy(k, c, t).wait_send()
            hy_copy(k, c, t).wait_send()
        for t in range(1, nz):
            z_copy(k, c, t).wait_send()
            hz_copy(k, c, t).wait_send()
        pair_copy(k, c).wait_recv()
        x_v[c] = (x_v[c].astype(jnp.float32) + (summed + pair_in[k * CHUNKS + c])).astype(jnp.bfloat16)
        pair_copy(k, c).wait_send()

        @pl.when(k + 1 < layers)
        def _():
            send_up(k + 1, c)

    for c in range(CHUNKS):
        send_up(0, c)

    def layer(k, carry):
        parts = [combine(k, c) for c in range(CHUNKS)]
        for c in range(CHUNKS):
            activate(k, c, *parts[c])
        sums = [forward(k, c) for c in range(CHUNKS)]
        for c in range(CHUNKS):
            finish(k, c, sums[c])
        return carry

    lax.fori_loop(0, layers, layer, 0)

    half = rows // 2
    spot = lax.broadcasted_iota(jnp.int32, (n * half, 1), 0)
    rank = rank_of(m * (streams // 2) + spot // frames % (streams // 2), spot // half * frames + spot % frames)
    slot = lax.broadcasted_iota(jnp.int32, (n * half, live), 1)
    place = jnp.where(slot == rank, 1.0, 0.0).astype(jnp.bfloat16)
    spread = jnp.dot(place, x_v[...].reshape(live, dq), preferred_element_type=jnp.float32).astype(jnp.bfloat16)
    fin_out[...] = spread.reshape(fin_out.shape)
    fin_in[0] = fin_out[s]
    copies = []
    for d in range(1, n):
        dest = lax.rem(s + d, n)
        copies.append(remote(fin_out.at[dest], fin_in.at[d], fs.at[d], fr.at[d], dest, m))
        copies[-1].start()
    out_ref[:, pl.ds(pl.multiple_of(s * dq, dq), dq)] = fin_in[0]
    for d in range(1, n):
        copies[d - 1].wait_recv()
        src = lax.rem(s - d + n, n)
        out_ref[:, pl.ds(pl.multiple_of(src * dq, dq), dq)] = fin_in[d]
    for c in copies:
        c.wait_send()


def run_layers(tokens, lengths, up_weight, down_weight, live):
    streams, frames, half = tokens.shape
    n = lax.axis_size("seq")
    layers, dq, ff = up_weight.shape
    fq = ff // n
    nz = n // 2
    width = dq * n
    rows = streams * frames
    sizes = (n, layers, streams, frames, live, dq, fq, width)
    ch = live // CHUNKS
    slots = layers * CHUNKS
    bf, f32, dma = jnp.bfloat16, jnp.float32, pltpu.SemaphoreType.DMA
    vmem = pl.BlockSpec(memory_space=pltpu.VMEM)
    hbm = pl.BlockSpec(memory_space=pltpu.HBM)
    lanes = -(-ch // 128) * 128
    out = pl.pallas_call(
        partial(exchange_kernel, sizes),
        out_shape=jax.ShapeDtypeStruct((rows // 2, width), bf),
        in_specs=[pl.BlockSpec(memory_space=pltpu.SMEM), vmem, hbm, hbm],
        out_specs=vmem,
        scratch_shapes=[
            pltpu.VMEM((layers, dq, ff), bf),
            pltpu.VMEM((layers, dq, ff), bf),
            pltpu.VMEM((n, rows, dq), bf),
            pltpu.VMEM((CHUNKS, ch, dq), bf),
            pltpu.VMEM((CHUNKS, 16, lanes), f32),
            pltpu.VMEM((CHUNKS, nz, ch + 16, fq), bf),
            pltpu.VMEM((slots, nz, ch + 16, fq), bf),
            pltpu.VMEM((CHUNKS, nz, ch + 16, fq), bf),
            pltpu.VMEM((slots, nz, ch + 16, fq), bf),
            pltpu.VMEM((slots, 2, nz, ch, fq), bf),
            pltpu.VMEM((CHUNKS, ch, dq), f32),
            pltpu.VMEM((slots, ch, dq), f32),
            pltpu.VMEM((n, rows // 2, dq), bf),
            pltpu.VMEM((n, rows // 2, dq), bf),
            dma((layers,)), dma((layers,)),
            dma((n,)), dma((n,)),
            dma((slots, nz)), dma((slots, nz)),
            dma((slots, nz)), dma((slots, nz)),
            dma((slots, nz)), dma((slots, nz)),
            dma((slots, nz)), dma((slots, nz)),
            dma((slots,)), dma((slots,)),
            dma((n,)), dma((n,)),
        ],
        compiler_params=pltpu.CompilerParams(
            collective_id=0, has_side_effects=True, vmem_limit_bytes=60 * 1024 * 1024
        ),
        name="exchange",
    )(lengths, tokens.reshape(rows, half), up_weight, down_weight)
    return out.reshape(streams // 2, frames, width)


def body(signal, lengths, chan_weight, up_weight, down_weight):
    streams, channels, samples = signal.shape
    frames = samples // HOP
    dft_table = spectral_table(HOP)
    boundary = shifted(signal[:, :, :HOP], "seq", -1)
    local_part = jnp.dot(
        signal.reshape(streams, channels, frames, HOP), dft_table, precision=lax.Precision.HIGH
    )
    edge_part = jnp.dot(boundary, dft_table[:, 2 * HOP :], precision=lax.Precision.HIGH)
    following = jnp.concatenate([local_part[:, :, 1:, 2 * HOP :], edge_part[:, :, None, :]], axis=2)
    spectrum = local_part[..., : 2 * HOP] + following
    logpower = log_power(spectrum)
    embedded = jnp.einsum(
        "scfb,cbe->sfce", logpower, chan_weight, preferred_element_type=jnp.float32
    )
    embedded = embedded.reshape(streams, frames, channels * chan_weight.shape[2])
    shards = lax.axis_size("seq")
    live = (streams + 1) * frames * shards // 2
    blocks = (up_weight.shape[1], up_weight.shape[2] // shards)
    if lax.axis_size("mdl") == 2 and shards % 2 == 0 and all(b % 128 == 0 for b in blocks) and live % (16 * CHUNKS) == 0 and live // CHUNKS <= blocks[1]:
        return run_layers(embedded.astype(jnp.bfloat16), lengths, up_weight, down_weight, live)
    frame_index = lax.axis_index("seq") * frames + jnp.arange(frames, dtype=jnp.int32)
    live_mask = frame_index[None, :] < lengths[:, None]
    tokens = jnp.where(live_mask[:, :, None], embedded, 0.0).astype(jnp.bfloat16)
    rows = lax.all_gather(tokens.reshape(streams * frames, -1), "mdl", axis=1, tiled=True)
    state = lax.all_to_all(rows, "seq", split_axis=1, concat_axis=0, tiled=True)
    width = rows.shape[1]
    for layer in range(up_weight.shape[0]):
        state = apply_layer(state, up_weight[layer], down_weight[layer], width)
    rows = lax.all_to_all(state, "seq", split_axis=0, concat_axis=1, tiled=True)
    full_rows = rows.reshape(streams, frames, width)
    half_streams = streams // lax.axis_size("mdl")
    return lax.dynamic_slice_in_dim(
        full_rows, lax.axis_index("mdl") * half_streams, half_streams, 0
    )


def solution(mesh):
    return jax.shard_map(
        body,
        mesh=mesh,
        in_specs=(
            P("grp", "mdl", "seq"),
            P("grp"),
            P("mdl", None, None),
            P(None, "seq", "mdl"),
            P(None, "seq", "mdl"),
        ),
        out_specs=P(("grp", "mdl"), "seq", None),
        check_vma=False,
    )
```
